32 devices in a mesh: batch: 4 (over y, core), vocab: 8 (over z, x).
Axes of the slice: x: 2, y: 2, z: 4, core: 2. Of those that a mesh axis runs over, the one named last changes fastest.
Arguments:
- hidden: bfloat16 [32768, 768], P(('batch', 'vocab')), may hold values from -150 to 150, as said below
- dense_w: bfloat16 [768, 768], replicated, may hold values from -0.21875 to 0.21875
- dense_b: float32 [768], replicated, may hold values from -3 to 3
- norm_gain: float32 [768], replicated, may hold values from 0.5 to 1.5
- norm_bias: float32 [768], replicated, may hold values from -2 to 2
- vocabulary_weight: bfloat16 [768, 30720], P(None, 'vocab'), may hold values from -0.21875 to 0.21875
- vocabulary_bias: bfloat16 [30720], P('vocab'), may hold values from -5 to 5
- lengths: int32 [128], P('batch'), may hold values from 32 to 256
- term_ids: int32 [128, 128], P('batch'), may hold values from -1 to 30521, as said below
Outputs:
- vectors: float32 [128, 30720], P('batch', 'vocab')
- posting_weights: float32 [32, 26, 32], P(('batch', 'vocab'))
- posting_key_codes: int32 [32, 26, 32], P(('batch', 'vocab'))
The draws below stay inside these ranges and needn't reach their ends.
Inputs may be any that keep to these rules, and one draw needn't show every extreme that they name: `hidden`: the last encoder layer's states. `term_ids`: no term appears twice in one passage and every term is below 30522. Within the 32 passages of one batch shard, the terms t with one value of t // 3840 and one value of t % (32) number at most 26, and in every draw one owner t % (32) reaches 26 for every batch shard and every value of t // 3840.
All inputs are finite; a program needn't handle non-finite values.
Results may differ from the reference program's by a relative error of at most 0.0009.
Values may be sent and summed in bfloat16 or wider, within the bound.
No kernel may reach another device: no remote copies, remote signals or barrier semaphores. Data moves between devices by JAX's collectives and lax.ppermute only.
A program may use at most 64 MiB of HBM per device.

```python
import jax
import jax.numpy as jnp
from jax import lax

MODEL_WIDTH = 768
VOCAB = 30522
VOCAB_PADDED = 30720
L = 256
K = 128
PB = 32
PAS = 128
TOKENS = 32768
POSTING_LIMIT = 26
N_BATCH = 4
N_VOCAB = 8


def draw_hidden(key, part):
    streams = jax.random.split(jax.random.fold_in(key, 5), 3)
    row_scales = jnp.exp(jax.random.uniform(streams[1], (TOKENS, 1), jnp.float32, jnp.log(0.5), jnp.log(5.0)))
    column_scales = jnp.exp(jax.random.uniform(streams[2], (1, MODEL_WIDTH), jnp.float32, jnp.log(0.5), jnp.log(5.0)))
    basic = jax.random.normal(streams[0], (TOKENS, MODEL_WIDTH), jnp.float32)
    basic = jnp.clip(basic, -6.0, 6.0)
    return (basic * row_scales * column_scales).astype(jnp.bfloat16)


def shard_terms(shard_key, hot_owner, boosts):
    device_list = N_BATCH * N_VOCAB
    owner_extent = VOCAB_PADDED // N_VOCAB // device_list
    cells = N_VOCAB * device_list
    total = cells * POSTING_LIMIT
    streams = jax.random.split(shard_key, 4)
    entries = jnp.arange(total, dtype=jnp.int32)
    cell_index = entries // POSTING_LIMIT
    copy_index = entries % POSTING_LIMIT
    vocab_shard = cell_index // device_list
    owners = cell_index % device_list
    jitter = jax.random.randint(streams[0], (total,), 0, 1024)
    offsets = jax.random.randint(streams[1], (cells,), 0, owner_extent)
    limits = jnp.minimum(owner_extent, (VOCAB - owners - vocab_shard * owner_extent * device_list + device_list - 1) // device_list)
    residue = (offsets[cell_index] + copy_index) % limits
    terms = (vocab_shard * owner_extent + residue) * device_list + owners
    drawn = jitter + boosts[owners] + 2048 - jnp.minimum(copy_index * 300, 2047)
    scores = jnp.where(owners == hot_owner, 3584 + jitter, drawn) * 32768 + entries
    chosen = lax.top_k(scores, PB * K)[1]
    kept = jax.random.randint(streams[2], (), PB * K * 3 // 4, PB * K + 1)
    ranked = jnp.where(jnp.arange(PB * K) < kept, terms[chosen], -1)
    shuffle = jax.random.permutation(streams[3], PB * K)
    return ranked[shuffle].reshape(PB, K)


def draw_term_ids(key, part):
    pieces = jax.random.split(jax.random.fold_in(key, 17), N_BATCH + 2)
    hot_owner = jax.random.randint(pieces[0], (), 0, N_BATCH * N_VOCAB)
    boosts = jax.random.randint(pieces[1], (N_BATCH * N_VOCAB,), 0, 512)
    shards = jax.vmap(lambda shard_key: shard_terms(shard_key, hot_owner, boosts))(pieces[2:])
    return shards.reshape(N_BATCH * PB, K).astype(jnp.int32)


def touch_ends(drawn, stream_key, low, top_value):
    dims = drawn.shape
    index_at = [jax.random.randint(jax.random.fold_in(stream_key, axis), (), 0, dims[axis]) for axis in range(len(dims))]
    drawn = drawn.at[tuple(index_at)].set(low)
    longest = dims.index(max(dims))
    index_at[longest] = (index_at[longest] + 1) % dims[longest]
    return drawn.at[tuple(index_at)].set(top_value)


def steps_of(stream_key, dims, cuts, smallest, high):
    def one(dim, parts):
        draws = jax.random.uniform(jax.random.fold_in(jax.random.fold_in(stream_key, 6), dim), (parts,), jnp.float32, smallest / len(cuts), high / len(cuts))
        return jnp.repeat(jnp.exp(draws), dims[dim] // parts).reshape((-1,) + (1,) * (len(dims) - dim - 1))

    factor_of = one(*cuts[0])
    for cut in cuts[1:]:
        factor_of = factor_of * one(*cut)
    return factor_of


def bell_draw(own_key, dims, scale, reach, cuts=(), held_as=jnp.bfloat16):
    values = scale * jax.random.normal(own_key, dims, jnp.float32)
    if cuts:
        values = values * steps_of(own_key, dims, cuts, -0.22, 0.18)
    return jnp.clip(values, -reach, reach).astype(held_as)


def setup_inputs(seed: int = 0) -> dict:
    splits = jax.random.split(jax.random.key(seed), 10)
    return {
        "hidden": draw_hidden(jax.random.fold_in(splits[9], 71), 0),
        "dense_w": bell_draw(splits[1], (MODEL_WIDTH, MODEL_WIDTH), MODEL_WIDTH ** -0.5, 0.21875),
        "dense_b": bell_draw(splits[2], (MODEL_WIDTH,), 0.5, 3.0, (), jnp.float32),
        "norm_gain": jnp.clip(1.0 + 0.1 * jax.random.normal(splits[3], (MODEL_WIDTH,), jnp.float32), 0.5, 1.5),
        "norm_bias": bell_draw(splits[4], (MODEL_WIDTH,), 0.3, 2.0, (), jnp.float32),
        "vocabulary_weight": bell_draw(splits[5], (MODEL_WIDTH, VOCAB_PADDED), MODEL_WIDTH ** -0.5, 0.21875, ((1, 8),)),
        "vocabulary_bias": bell_draw(splits[6], (VOCAB_PADDED,), 1.0, 5.0, ((0, 8),)),
        "lengths": touch_ends(jax.random.randint(splits[7], (PAS,), L // 8, L + 1), jax.random.fold_in(splits[7], 1), L // 8, L).astype(jnp.int32),
        "term_ids": draw_term_ids(jax.random.fold_in(splits[9], 71), 0),
    }


def transform_rows(token_rows, dense_w, dense_b, norm_gain, norm_bias):
    pre = jnp.dot(token_rows, dense_w, preferred_element_type=jnp.float32) + dense_b
    activated = jax.nn.gelu(pre, approximate=False)
    centered = activated - lax.optimization_barrier(jnp.mean(activated, axis=-1, keepdims=True))
    spread = lax.optimization_barrier(jnp.mean(centered * centered, axis=-1, keepdims=True))
    normed = centered * lax.rsqrt(spread + 1e-06) * norm_gain + norm_bias
    return normed.astype(jnp.bfloat16)

def reference(hidden, dense_w, dense_b, norm_gain, norm_bias, vocabulary_weight, vocabulary_bias, lengths, term_ids):
    passage_rows = hidden.reshape(PAS, L, MODEL_WIDTH)
    positions = jnp.arange(L).astype(jnp.int32)
    bias_wide = vocabulary_bias.astype(jnp.float32)

    def one_passage(passage_pair):
        token_rows, length = passage_pair
        normed = transform_rows(token_rows, dense_w, dense_b, norm_gain, norm_bias)
        logits = jnp.dot(normed, vocabulary_weight, preferred_element_type=jnp.float32) + bias_wide
        active = jnp.log1p(jnp.maximum(logits, 0.0))
        counted = (positions < length)[:, None]
        return lax.optimization_barrier(jnp.max(jnp.where(counted, active, 0.0), axis=0))
    vectors = lax.map(one_passage, (passage_rows, lengths))
    column_span = jnp.arange(VOCAB_PADDED).astype(jnp.int32)
    vectors = jnp.where(column_span[None, :] < VOCAB, vectors, 0.0)
    device_list = N_BATCH * N_VOCAB
    owner_width = VOCAB_PADDED // N_VOCAB
    flattened_terms = term_ids.reshape(-1)
    present = flattened_terms >= 0
    clamped_terms = jnp.where(present, flattened_terms, 0).astype(jnp.int32)
    passage_position = (jnp.arange(PAS * K) // K).astype(jnp.int32)
    picked = vectors[passage_position, clamped_terms]
    owners = (clamped_terms % device_list).astype(jnp.int32)
    sender_ids = (passage_position // PB * N_VOCAB + clamped_terms // owner_width).astype(jnp.int32)
    groups = sender_ids * device_list + owners

    def count_step(totals, group_pair):
        group_id, alive_flag = group_pair
        placed = totals[group_id]
        return (totals.at[group_id].add(alive_flag.astype(jnp.int32)), placed)
    finals, posting_slots = lax.scan(count_step, jnp.zeros((device_list * device_list,), jnp.int32), (groups, present))
    receiver_ids = jnp.where(present, owners, device_list).astype(jnp.int32)
    posting_weights = jnp.zeros((device_list, POSTING_LIMIT, device_list), jnp.float32).at[receiver_ids, posting_slots, sender_ids].set(picked, mode='drop')
    posting_key_codes = jnp.full((device_list, POSTING_LIMIT, device_list), -1, jnp.int32).at[receiver_ids, posting_slots, sender_ids].set((passage_position * VOCAB_PADDED + clamped_terms).astype(jnp.int32), mode='drop')
    return (vectors, posting_weights, posting_key_codes)
```

```python
import functools

import jax
import jax.numpy as jnp
from jax import lax
from jax.experimental import pallas as pl
from jax.experimental.pallas import tpu as pltpu
from jax.sharding import PartitionSpec as P

VOCAB = 30522
VOCAB_PADDED = 30720
L = 256
K = 128
TILE = 32
BLOCK = 256
LANES = 128
LOW = -3.0e38
F32 = jnp.float32


def full(shape):
    return pl.BlockSpec(shape, lambda *_: (0,) * len(shape))


def dense_kernel(lens, x_ref, w_ref, b_ref, gain_ref, bias_ref, o_ref, rows_ref, pre_ref, *, first, tile):
    passages = x_ref.shape[0] // L
    rows = o_ref.shape[0]
    starts, ends = [], []
    total = jnp.int32(0)
    for p in range(passages):
        starts.append(total)
        total = total + lax.div(lens[p] + (tile - 1), jnp.int32(tile))
        ends.append(total)
    base = first // tile
    counts = []
    for i in range(rows // tile):
        slot = jnp.int32(base + i)
        source, begin, length = jnp.int32(0), jnp.int32(0), lens[0]
        for p in range(1, passages):
            later = slot >= ends[p - 1]
            source = jnp.where(later, p, source)
            begin = jnp.where(later, starts[p], begin)
            length = jnp.where(later, lens[p], length)
        inner = jnp.clip((slot - begin) * tile, 0, L - tile)
        counts.append(length - inner)
        at = pl.multiple_of(source * L + inner, tile)
        rows_ref[i * tile : (i + 1) * tile, :] = x_ref[pl.ds(at, tile), :]

    @pl.when(base < total)
    def _():
        pre_ref[...] = jnp.dot(rows_ref[...], w_ref[...], preferred_element_type=F32) + b_ref[...]
        for i in range(rows // tile):

            @pl.when(base + i < total)
            def _(i=i):
                pre = pre_ref[i * tile : (i + 1) * tile, :]
                act = 0.5 * pre * (1.0 + lax.erf(pre * 0.7071067811865476))
                width = act.shape[1]
                centered = act - jnp.sum(act, axis=1, keepdims=True) * (1.0 / width)
                spread = jnp.sum(centered * centered, axis=1, keepdims=True) * (1.0 / width)
                normed = centered * lax.rsqrt(spread + 1e-06) * gain_ref[...] + bias_ref[...]
                at = lax.broadcasted_iota(jnp.int32, normed.shape, 0)
                normed = jnp.where(at < counts[i], normed, normed[0:1, :])
                o_ref[i * tile : (i + 1) * tile, :] = normed.astype(o_ref.dtype)


def dense(lens, x, w, b, gain, bias, first, rows, tile):
    width = x.shape[1]
    return pl.pallas_call(
        functools.partial(dense_kernel, first=first, tile=tile),
        out_shape=jax.ShapeDtypeStruct((rows, width), x.dtype),
        grid_spec=pltpu.PrefetchScalarGridSpec(
            num_scalar_prefetch=1,
            grid=(1,),
            in_specs=[full(x.shape), full(w.shape), full(b.shape), full(gain.shape), full(bias.shape)],
            out_specs=full((rows, width)),
            scratch_shapes=[pltpu.VMEM((rows, width), x.dtype), pltpu.VMEM((rows, width), F32)],
        ),
        compiler_params=pltpu.CompilerParams(vmem_limit_bytes=24 << 20),
        cost_estimate=pl.CostEstimate(
            flops=2 * rows * width * width, bytes_accessed=2 * (rows * width * 2 + width * width), transcendentals=rows * width
        ),
        name="dense",
    )(lens, x, w, b, gain, bias)


def pool_kernel(live, seg, *refs, tile, block, count):
    rows_refs, w_ref, o_ref, acc = refs[:count], refs[count], refs[count + 1], refs[count + 2]
    passages = o_ref.shape[0]
    acc[...] = jnp.full(acc.shape, LOW, F32)
    width = w_ref.shape[1]

    def one(ref, at, index):
        @pl.when(live[index] > 0)
        def _():
            got = jnp.dot(ref[pl.ds(at, block), :], w_ref[...], preferred_element_type=F32)
            for t in range(block // tile):
                s = seg[index * (block // tile) + t]
                part = jnp.max(got[t * tile : (t + 1) * tile].reshape(tile // 8, 8, width), axis=0)
                acc[s] = jnp.maximum(acc[s], part)

    index = 0
    for ref in rows_refs:
        blocks = ref.shape[0] // block
        if blocks == 1:
            one(ref, 0, index)
        else:

            def step(i, _, ref=ref, index=index):
                one(ref, pl.multiple_of(i * block, block), index + i)
                return 0

            lax.fori_loop(0, blocks, step, 0)
        index += blocks
    o_ref[...] = jnp.max(acc[:passages], axis=1)


def pool(live, seg, rows, w, passages, tile, block, columns):
    depth, width = w.shape
    total = sum(r.shape[0] for r in rows)
    return pl.pallas_call(
        functools.partial(pool_kernel, tile=tile, block=block, count=len(rows)),
        out_shape=jax.ShapeDtypeStruct((passages, width), F32),
        grid_spec=pltpu.PrefetchScalarGridSpec(
            num_scalar_prefetch=2,
            grid=(width // columns,),
            in_specs=[pl.BlockSpec(r.shape, lambda *_: (0, 0), pipeline_mode=pl.Buffered(1)) for r in rows]
            + [pl.BlockSpec((depth, columns), lambda j, *_: (0, j))],
            out_specs=pl.BlockSpec((passages, columns), lambda j, *_: (0, j)),
            scratch_shapes=[pltpu.VMEM((passages + 1, 8, columns), F32)],
        ),
        compiler_params=pltpu.CompilerParams(vmem_limit_bytes=40 << 20),
        cost_estimate=pl.CostEstimate(
            flops=2 * total * depth * width, bytes_accessed=2 * (total * depth + depth * width), transcendentals=0
        ),
        name="pool",
    )(live, seg, *rows, w)


def slots_kernel(where_ref, ids_ref, s_ref, k_ref, *, owners, capacity, width):
    terms, passages = ids_ref.shape
    shard, first_passage = where_ref[0], where_ref[1]
    lower = (
        lax.broadcasted_iota(jnp.int32, (terms, terms), 1) < lax.broadcasted_iota(jnp.int32, (terms, terms), 0)
    ).astype(jnp.bfloat16)
    tiles = s_ref.shape[0]
    owner_lane = lax.broadcasted_iota(jnp.int32, (terms, LANES), 1)
    tile_lane = lax.broadcasted_iota(jnp.int32, (terms, tiles), 1)
    seen = jnp.zeros((1, LANES), F32)
    for p in range(passages):
        ids = ids_ref[:, p : p + 1]
        column = ids - shard * width
        mine = (ids >= 0) & (column >= 0) & (column < width)
        column = jnp.where(mine, column, -1)
        owner = jnp.where(mine, jnp.bitwise_and(ids, owners - 1), -1)
        hot = (owner_lane == owner).astype(F32)
        before = jnp.dot(lower, hot.astype(jnp.bfloat16), preferred_element_type=F32) + seen
        place = jnp.sum(hot * before, axis=1, keepdims=True) + 1.0
        seen = seen + jnp.sum(hot, axis=0, keepdims=True)
        row_tile = jnp.where(mine, lax.shift_right_logical(jnp.maximum(column, 0), 7), -1)
        lane = jnp.bitwise_and(jnp.maximum(column, 0), LANES - 1)
        left = jnp.where(tile_lane == row_tile, place, 0.0).astype(jnp.bfloat16)
        right = (owner_lane == lane).astype(jnp.bfloat16)
        s_ref[:, p, :] = lax.dot_general(left, right, (((0,), (0,)), ((), ())), preferred_element_type=F32)

    def step(j, totals):
        place = s_ref[j]
        code = (
            (first_passage + lax.broadcasted_iota(jnp.int32, place.shape, 0)) * VOCAB_PADDED
            + (shard * width + j * LANES + 1)
            + lax.broadcasted_iota(jnp.int32, place.shape, 1)
        )
        return tuple(
            total + fold8(jnp.where(place == float(c + 1), code, 0)) for c, total in enumerate(totals)
        )

    totals = lax.fori_loop(0, tiles, step, tuple(jnp.zeros((8, LANES), jnp.int32) for _ in range(capacity)))
    for c in range(capacity):
        k_ref[c : c + 1, :] = fold_lanes(jnp.sum(totals[c], axis=0, keepdims=True), owners) - 1


def fold8(x):
    total = x[0:8]
    for i in range(8, x.shape[0], 8):
        total = total + x[i : i + 8]
    return total


def fold_lanes(row, owners):
    total = row[:, 0:owners]
    for i in range(owners, LANES, owners):
        total = total + row[:, i : i + owners]
    return total


def slots(where, ids_t, owners, capacity, width):
    terms, passages = ids_t.shape
    tiles = width // LANES
    return pl.pallas_call(
        functools.partial(slots_kernel, owners=owners, capacity=capacity, width=width),
        out_shape=(
            jax.ShapeDtypeStruct((tiles, passages, LANES), F32),
            jax.ShapeDtypeStruct((capacity, owners), jnp.int32),
        ),
        grid_spec=pltpu.PrefetchScalarGridSpec(
            num_scalar_prefetch=1,
            grid=(1,),
            in_specs=[full(ids_t.shape)],
            out_specs=(full((tiles, passages, LANES)), full((capacity, owners))),
        ),
        compiler_params=pltpu.CompilerParams(vmem_limit_bytes=16 << 20),
        cost_estimate=pl.CostEstimate(flops=1 << 26, bytes_accessed=1 << 20, transcendentals=0),
        name="slots",
    )(where, ids_t)


def finish_kernel(where_ref, *refs, count, owners):
    pooled, bias_ref, s_ref, v_ref, t_ref = refs[:count], refs[count], refs[count + 1], refs[count + 2], refs[count + 3]
    passages, width = v_ref.shape
    capacity = t_ref.shape[0]
    totals = [jnp.zeros((8, LANES), F32) for _ in range(capacity)]
    for j in range(width // LANES):
        at = slice(j * LANES, (j + 1) * LANES)
        top = pooled[0][:, at]
        for ref in pooled[1:]:
            top = jnp.maximum(top, ref[:, at])
        value = jnp.log1p(jnp.maximum(top + bias_ref[:, at].astype(F32), 0.0))
        column = where_ref[0] * width + j * LANES + lax.broadcasted_iota(jnp.int32, value.shape, 1)
        value = jnp.where(column < VOCAB, value, 0.0)
        v_ref[:, at] = value
        place = s_ref[j]
        totals = [t + fold8(jnp.where(place == float(c + 1), value, 0.0)) for c, t in enumerate(totals)]
    for c in range(capacity):
        t_ref[c : c + 1, :] = fold_lanes(jnp.sum(totals[c], axis=0, keepdims=True), owners)


def finish(where, pooled, bias, places, first, owners, capacity):
    passages, width = pooled[0].shape
    tiles = width // LANES
    return pl.pallas_call(
        functools.partial(finish_kernel, count=len(pooled), owners=owners),
        out_shape=(
            jax.ShapeDtypeStruct((passages, width), F32),
            jax.ShapeDtypeStruct((capacity, owners), F32),
        ),
        grid_spec=pltpu.PrefetchScalarGridSpec(
            num_scalar_prefetch=1,
            grid=(1,),
            in_specs=[full(p.shape) for p in pooled]
            + [full(bias.shape), pl.BlockSpec((tiles, passages, LANES), lambda i, where: (0, where[1], 0))],
            out_specs=(full((passages, width)), full((capacity, owners))),
        ),
        compiler_params=pltpu.CompilerParams(vmem_limit_bytes=24 << 20),
        cost_estimate=pl.CostEstimate(flops=1 << 24, bytes_accessed=1 << 20, transcendentals=passages * width),
        name="finish",
    )(where, *pooled, bias, places)


def tables(lens, group_passages, tile, rows):
    groups, per = lens.shape
    need = (lens + (tile - 1)) // tile
    slot = jnp.arange(rows // tile, dtype=jnp.int32)[None, :]
    index = jnp.zeros((groups, rows // tile), jnp.int32)
    total = jnp.zeros((groups, 1), jnp.int32)
    for p in range(per):
        total = total + need[:, p : p + 1]
        index = index + (slot >= total).astype(jnp.int32)
    passage = jnp.arange(groups, dtype=jnp.int32)[:, None] * per + index
    return total[:, 0], jnp.where(index < per, passage, group_passages)


def local(
    hidden,
    dense_w,
    dense_b,
    norm_gain,
    norm_bias,
    vocabulary_weight,
    vocabulary_bias,
    lengths,
    term_ids,
):
    passages = lengths.shape[0]
    width = vocabulary_weight.shape[1]
    rows = hidden.shape[0]
    mine = rows // L
    vocab_count = lax.axis_size("vocab")
    batch_count = lax.axis_size("batch")
    owners = vocab_count * batch_count
    capacity = 3 * passages * K // (2 * vocab_count * owners) + 2
    shard = lax.axis_index("vocab")
    batch = lax.axis_index("batch")

    own_lens = lax.dynamic_slice(lengths, (shard * mine,), (mine,))
    normed = dense(
        own_lens, hidden, dense_w, dense_b[None], norm_gain[None], norm_bias[None], 0, rows, TILE
    )
    gathered = lax.all_gather(normed, "vocab", axis=0, tiled=True)

    where = jnp.stack([shard, batch * passages]).astype(jnp.int32)
    places, send_keys = slots(where, term_ids.T, owners, capacity, width)
    got_keys = lax.all_to_all(send_keys, ("batch", "vocab"), split_axis=1, concat_axis=1, tiled=True)

    live, seg = tables(lengths.reshape(vocab_count, mine), passages, TILE, rows)
    begin = jnp.arange(rows // BLOCK, dtype=jnp.int32)[None, :] * (BLOCK // TILE)
    live = (live[:, None] > begin).astype(jnp.int32)
    columns = width // 5
    pooled = pool(live.reshape(-1), seg.reshape(-1), [gathered], vocabulary_weight, passages, TILE, BLOCK, columns)
    vectors, send_weights = finish(
        jnp.stack([shard, 0 * shard]).astype(jnp.int32), [pooled], vocabulary_bias[None], places, 0, owners, capacity
    )
    got_weights = lax.all_to_all(send_weights, ("batch", "vocab"), split_axis=1, concat_axis=1, tiled=True)
    return vectors, got_weights[None], got_keys[None]


def solution(mesh):
    in_specs = (
        P(("batch", "vocab"), None),
        P(),
        P(),
        P(),
        P(),
        P(None, "vocab"),
        P("vocab"),
        P("batch"),
        P("batch", None),
    )
    out_specs = (
        P("batch", "vocab"),
        P(("batch", "vocab"), None, None),
        P(("batch", "vocab"), None, None),
    )
    return jax.shard_map(local, mesh=mesh, in_specs=in_specs, out_specs=out_specs, check_vma=False)
```

```python
import functools

import jax
import jax.numpy as jnp
from jax import lax
from jax.experimental import pallas as pl
from jax.experimental.pallas import tpu as pltpu
from jax.sharding import PartitionSpec as P


VOCAB = 30522
VOCAB_PADDED = 30720
L = 256
K = 128
TILE = 32
BLOCK = 256
LANES = 128
LOW = -3.0e38
F32 = jnp.float32


def full(shape):
    return pl.BlockSpec(shape, lambda *_: (0,) * len(shape))


def dense_kernel(lens, x_ref, w_ref, b_ref, gain_ref, bias_ref, o_ref, rows_ref, pre_ref, *, first, tile):
    passages = x_ref.shape[0] // L
    rows = o_ref.shape[0]
    starts, ends = [], []
    total = jnp.int32(0)
    for p in range(passages):
        starts.append(total)
        total = total + lax.div(lens[p] + (tile - 1), jnp.int32(tile))
        ends.append(total)
    base = first // tile
    counts = []
    for i in range(rows // tile):
        slot = jnp.int32(base + i)
        source, begin, length = jnp.int32(0), jnp.int32(0), lens[0]
        for p in range(1, passages):
            later = slot >= ends[p - 1]
            source = jnp.where(later, p, source)
            begin = jnp.where(later, starts[p], begin)
            length = jnp.where(later, lens[p], length)
        inner = jnp.clip((slot - begin) * tile, 0, L - tile)
        counts.append(length - inner)
        at = pl.multiple_of(source * L + inner, tile)
        rows_ref[i * tile : (i + 1) * tile, :] = x_ref[pl.ds(at, tile), :]

    @pl.when(base < total)
    def _():
        pre_ref[...] = jnp.dot(rows_ref[...], w_ref[...], preferred_element_type=F32) + b_ref[...]
        for i in range(rows // tile):

            @pl.when(base + i < total)
            def _(i=i):
                pre = pre_ref[i * tile : (i + 1) * tile, :]
                act = 0.5 * pre * (1.0 + lax.erf(pre * 0.7071067811865476))
                width = act.shape[1]
                centered = act - jnp.sum(act, axis=1, keepdims=True) * (1.0 / width)
                spread = jnp.sum(centered * centered, axis=1, keepdims=True) * (1.0 / width)
                normed = centered * lax.rsqrt(spread + 1e-06) * gain_ref[...] + bias_ref[...]
                at = lax.broadcasted_iota(jnp.int32, normed.shape, 0)
                normed = jnp.where(at < counts[i], normed, normed[0:1, :])
                o_ref[i * tile : (i + 1) * tile, :] = normed.astype(o_ref.dtype)


def dense(lens, x, w, b, gain, bias, first, rows, tile):
    width = x.shape[1]
    return pl.pallas_call(
        functools.partial(dense_kernel, first=first, tile=tile),
        out_shape=jax.ShapeDtypeStruct((rows, width), x.dtype),
        grid_spec=pltpu.PrefetchScalarGridSpec(
            num_scalar_prefetch=1,
            grid=(1,),
            in_specs=[full(x.shape), full(w.shape), full(b.shape), full(gain.shape), full(bias.shape)],
            out_specs=full((rows, width)),
            scratch_shapes=[pltpu.VMEM((rows, width), x.dtype), pltpu.VMEM((rows, width), F32)],
        ),
        compiler_params=pltpu.CompilerParams(vmem_limit_bytes=24 << 20),
        cost_estimate=pl.CostEstimate(
            flops=2 * rows * width * width, bytes_accessed=2 * (rows * width * 2 + width * width), transcendentals=rows * width
        ),
        name="dense",
    )(lens, x, w, b, gain, bias)


def pool_kernel(live, seg, *refs, tile, block, count):
    rows_refs, w_ref, o_ref, packed, acc, owner, total = refs[:count], *refs[count:]
    passages = o_ref.shape[0]

    @pl.when(pl.program_id(0) == 0)
    def _():
        filled = jnp.int32(0)
        index = 0
        for g, ref in enumerate(rows_refs):
            tiles = ref.shape[0] // tile
            alive = jnp.clip(live[g], 0, tiles)

            def take(i, at, ref=ref, index=index):
                packed[pl.ds(pl.multiple_of(at * tile, tile), tile), :] = ref[
                    pl.ds(pl.multiple_of(i * tile, tile), tile), :
                ]
                owner[at] = seg[index + i]
                return at + 1

            filled = lax.fori_loop(0, alive, take, filled)
            index += tiles
        total[0] = lax.div(filled + (block // tile - 1), jnp.int32(block // tile))
        for t in range(block // tile - 1):
            owner[filled + t] = passages

    acc[...] = jnp.full(acc.shape, LOW, F32)
    width = w_ref.shape[1]

    def step(b, _):
        got = jnp.dot(
            packed[pl.ds(pl.multiple_of(b * block, block), block), :], w_ref[...], preferred_element_type=F32
        )
        for t in range(block // tile):
            s = owner[b * (block // tile) + t]
            part = jnp.max(got[t * tile : (t + 1) * tile].reshape(tile // 8, 8, width), axis=0)
            acc[s] = jnp.maximum(acc[s], part)
        return 0

    lax.fori_loop(0, total[0], step, 0)
    o_ref[...] = jnp.max(acc[:passages], axis=1)


def pool(live, seg, rows, w, passages, tile, columns):
    depth, width = w.shape
    block = BLOCK
    total = sum(r.shape[0] for r in rows)
    return pl.pallas_call(
        functools.partial(pool_kernel, tile=tile, block=block, count=len(rows)),
        out_shape=jax.ShapeDtypeStruct((passages, width), F32),
        grid_spec=pltpu.PrefetchScalarGridSpec(
            num_scalar_prefetch=2,
            grid=(width // columns,),
            in_specs=[pl.BlockSpec(r.shape, lambda *_: (0, 0), pipeline_mode=pl.Buffered(1)) for r in rows]
            + [pl.BlockSpec((depth, columns), lambda j, *_: (0, j))],
            out_specs=pl.BlockSpec((passages, columns), lambda j, *_: (0, j)),
            scratch_shapes=[
                pltpu.VMEM((total + block, depth), w.dtype),
                pltpu.VMEM((passages + 1, 8, columns), F32),
                pltpu.SMEM(((total + block) // tile,), jnp.int32),
                pltpu.SMEM((1,), jnp.int32),
            ],
        ),
        compiler_params=pltpu.CompilerParams(vmem_limit_bytes=(16 << 20) + 4 * total * depth),
        cost_estimate=pl.CostEstimate(
            flops=2 * total * depth * width, bytes_accessed=2 * (total * depth + depth * width), transcendentals=0
        ),
        name="pool",
    )(live, seg, *rows, w)


def slots_kernel(where_ref, ids_ref, s_ref, *k_refs, owners, capacity, width):
    terms, passages = ids_ref.shape
    shard, first_passage = where_ref[0], where_ref[1]
    lower = (
        lax.broadcasted_iota(jnp.int32, (terms, terms), 1) < lax.broadcasted_iota(jnp.int32, (terms, terms), 0)
    ).astype(jnp.bfloat16)
    tiles = s_ref.shape[0]
    owner_lane = lax.broadcasted_iota(jnp.int32, (terms, LANES), 1)
    tile_lane = lax.broadcasted_iota(jnp.int32, (terms, tiles), 1)
    seen = jnp.zeros((1, LANES), F32)
    for p in range(passages):
        ids = ids_ref[:, p : p + 1]
        column = ids - shard * width
        mine = (ids >= 0) & (column >= 0) & (column < width)
        column = jnp.where(mine, column, -1)
        owner = jnp.where(mine, jnp.bitwise_and(ids, owners - 1), -1)
        hot = (owner_lane == owner).astype(F32)
        before = jnp.dot(lower, hot.astype(jnp.bfloat16), preferred_element_type=F32) + seen
        place = jnp.sum(hot * before, axis=1, keepdims=True) + 1.0
        seen = seen + jnp.sum(hot, axis=0, keepdims=True)
        row_tile = jnp.where(mine, lax.shift_right_logical(jnp.maximum(column, 0), 7), -1)
        lane = jnp.bitwise_and(jnp.maximum(column, 0), LANES - 1)
        left = jnp.where(tile_lane == row_tile, place, 0.0).astype(jnp.bfloat16)
        right = (owner_lane == lane).astype(jnp.bfloat16)
        s_ref[:, p, :] = lax.dot_general(left, right, (((0,), (0,)), ((), ())), preferred_element_type=F32)

    if not k_refs:
        return
    k_ref = k_refs[0]

    def step(j, totals):
        place = s_ref[j]
        code = (
            (first_passage + lax.broadcasted_iota(jnp.int32, place.shape, 0)) * VOCAB_PADDED
            + (shard * width + j * LANES + 1)
            + lax.broadcasted_iota(jnp.int32, place.shape, 1)
        )
        return tuple(
            total + fold8(jnp.where(place == float(c + 1), code, 0)) for c, total in enumerate(totals)
        )

    totals = lax.fori_loop(0, tiles, step, tuple(jnp.zeros((8, LANES), jnp.int32) for _ in range(capacity)))
    for c in range(capacity):
        k_ref[c : c + 1, :] = fold_lanes(jnp.sum(totals[c], axis=0, keepdims=True), owners) - 1


def fold8(x):
    total = x[0:8]
    for i in range(8, x.shape[0], 8):
        total = total + x[i : i + 8]
    return total


def fold_lanes(row, owners):
    total = row[:, 0:owners]
    for i in range(owners, LANES, owners):
        total = total + row[:, i : i + owners]
    return total


def slots(where, ids_t, owners, capacity, width, keys):
    terms, passages = ids_t.shape
    tiles = width // LANES
    shapes = [jax.ShapeDtypeStruct((tiles, passages, LANES), F32)]
    if keys:
        shapes.append(jax.ShapeDtypeStruct((capacity, owners), jnp.int32))
    return pl.pallas_call(
        functools.partial(slots_kernel, owners=owners, capacity=capacity, width=width),
        out_shape=shapes,
        grid_spec=pltpu.PrefetchScalarGridSpec(
            num_scalar_prefetch=1,
            grid=(1,),
            in_specs=[full(ids_t.shape)],
            out_specs=[full(x.shape) for x in shapes],
        ),
        compiler_params=pltpu.CompilerParams(vmem_limit_bytes=16 << 20),
        cost_estimate=pl.CostEstimate(flops=1 << 26, bytes_accessed=1 << 20, transcendentals=0),
        name="slots",
    )(where, ids_t)


def finish_kernel(where_ref, *refs, count, owners):
    pooled, bias_ref, s_ref, v_ref, t_ref = refs[:count], refs[count], refs[count + 1], refs[count + 2], refs[count + 3]
    passages, width = v_ref.shape
    capacity = t_ref.shape[0]
    totals = [jnp.zeros((8, LANES), F32) for _ in range(capacity)]
    for j in range(width // LANES):
        at = slice(j * LANES, (j + 1) * LANES)
        top = pooled[0][:, at]
        for ref in pooled[1:]:
            top = jnp.maximum(top, ref[:, at])
        value = jnp.log1p(jnp.maximum(top + bias_ref[:, at].astype(F32), 0.0))
        column = where_ref[0] * width + j * LANES + lax.broadcasted_iota(jnp.int32, value.shape, 1)
        value = jnp.where(column < VOCAB, value, 0.0)
        v_ref[:, at] = value
        place = s_ref[j]
        totals = [t + fold8(jnp.where(place == float(c + 1), value, 0.0)) for c, t in enumerate(totals)]
    for c in range(capacity):
        t_ref[c : c + 1, :] = fold_lanes(jnp.sum(totals[c], axis=0, keepdims=True), owners)


def finish(where, pooled, bias, places, owners, capacity):
    passages, width = pooled[0].shape
    tiles = width // LANES
    return pl.pallas_call(
        functools.partial(finish_kernel, count=len(pooled), owners=owners),
        out_shape=(
            jax.ShapeDtypeStruct((passages, width), F32),
            jax.ShapeDtypeStruct((capacity, owners), F32),
        ),
        grid_spec=pltpu.PrefetchScalarGridSpec(
            num_scalar_prefetch=1,
            grid=(1,),
            in_specs=[full(p.shape) for p in pooled]
            + [full(bias.shape), pl.BlockSpec((tiles, passages, LANES), lambda i, where: (0, where[1], 0))],
            out_specs=(full((passages, width)), full((capacity, owners))),
        ),
        compiler_params=pltpu.CompilerParams(vmem_limit_bytes=24 << 20),
        cost_estimate=pl.CostEstimate(flops=1 << 24, bytes_accessed=1 << 20, transcendentals=passages * width),
        name="finish",
    )(where, *pooled, bias, places)


def tables(lens, group_passages, tile, rows):
    groups, per = lens.shape
    need = (lens + (tile - 1)) // tile
    slot = jnp.arange(rows // tile, dtype=jnp.int32)[None, :]
    index = jnp.zeros((groups, rows // tile), jnp.int32)
    total = jnp.zeros((groups, 1), jnp.int32)
    for p in range(per):
        total = total + need[:, p : p + 1]
        index = index + (slot >= total).astype(jnp.int32)
    passage = jnp.arange(groups, dtype=jnp.int32)[:, None] * per + index
    return total[:, 0], jnp.where(index < per, passage, group_passages)


def gather_plan(hidden, weights, norms, vocabulary_weight, vocabulary_bias, lengths, places, own, owners, capacity):
    passages = lengths.shape[0]
    width = vocabulary_weight.shape[1]
    rows = hidden.shape[0]
    mine = rows // L
    vocab_count = lax.axis_size("vocab")
    shard = lax.axis_index("vocab")
    own_lens = lax.dynamic_slice(lengths, (shard * mine,), (mine,))
    normed = dense(own_lens, hidden, *weights, *norms, 0, rows, TILE)
    gathered = lax.all_gather(normed, "vocab", axis=0, tiled=True)
    live, seg = tables(lengths.reshape(vocab_count, mine), passages, TILE, rows)
    blocks = [gathered[i * rows : (i + 1) * rows] for i in range(vocab_count)]
    half = vocab_count // 2
    pooled = [
        pool(live[i : i + half], seg[i : i + half].reshape(-1), blocks[i : i + half], vocabulary_weight, passages, TILE, width // 5)
        for i in (0, half)
    ]
    vectors, sent = finish(
        jnp.stack([shard, 0 * shard]).astype(jnp.int32), pooled, vocabulary_bias[None], places[own], owners, capacity
    )
    return vectors, exchange(sent)


def exchange(table):
    return lax.all_to_all(table, ("batch", "vocab"), split_axis=1, concat_axis=1, tiled=True)


def tie(value, after):
    return lax.optimization_barrier((value, after))[0]


def pairs(moves, inner):
    return [(a * inner + i, b * inner + i) for a, b in moves for i in range(inner)]


INNER = 2
NEAR = pairs([(0, 0), (1, 2), (2, 1), (3, 3)], INNER)
FAR = pairs([(2, 3), (1, 0), (3, 1), (0, 2)], INNER)
ACROSS = [(v, v ^ 1) for v in range(8)]
BESIDE = [(v, v ^ 2) for v in range(8)]
SOURCES = [[2 * z + x for x in (i, 1 - i) for z in (a, b)] for a, b in ((0, 1), (2, 3), (1, 0), (3, 2)) for i in (0, 1)]
PIECES = 2
BATCH_OUTER = [(b, b ^ 2) for b in range(4)]
BATCH_INNER = [(b, b ^ 1) for b in range(4)]
SHARES = (0.25, 0.25, 0.25, 0.125, 0.125)


def quad_plan(hidden, weights, norms, vocabulary_weight, vocabulary_bias, lengths, places, own, owners, capacity):
    depth, width = vocabulary_weight.shape
    rows = hidden.shape[0]
    mine = rows // L
    quad = 4 * mine
    shard = lax.axis_index("vocab")
    batch = lax.axis_index("batch")
    upper = jnp.bitwise_and(lax.shift_right_logical(shard, 1), 1)

    quarter = depth // 4
    step = quarter // PIECES
    other_weight = jnp.zeros((depth, width), vocabulary_weight.dtype)
    before = None
    for i in range(PIECES):
        part = lax.dynamic_slice(vocabulary_weight, (batch * quarter + i * step, 0), (step, width))
        if before is not None:
            part = tie(part, before)
        a = lax.ppermute(part, "vocab", BESIDE)
        b = lax.ppermute(a, "batch", BATCH_OUTER)
        c = lax.ppermute(a, "batch", BATCH_INNER)
        d = lax.ppermute(b, "batch", BATCH_INNER)
        before = a
        for piece, index in ((a, batch), (b, batch ^ 2), (c, batch ^ 1), (d, batch ^ 3)):
            other_weight = lax.dynamic_update_slice(other_weight, piece, (index * quarter + i * step, 0))
    other_bias = lax.ppermute(vocabulary_bias, "vocab", BESIDE)

    sources = lax.dynamic_index_in_dim(jnp.array(SOURCES, jnp.int32), shard, 0, keepdims=False)
    by_block = lengths.reshape(-1, mine)
    group_lens = jnp.concatenate([lax.dynamic_slice(by_block, (sources[g], 0), (1, mine)) for g in range(4)], axis=0)
    live, seg = tables(group_lens, quad, TILE, rows)
    offset = (jnp.bitwise_and(sources, 3) - jnp.arange(4, dtype=jnp.int32)) * mine
    seg = jnp.where(seg < quad, seg + offset[:, None], quad)

    own_lens = lax.dynamic_slice(lengths, (shard * mine,), (mine,))
    chunks = [int(share * rows) for share in SHARES]
    firsts = [sum(chunks[:k]) for k in range(len(chunks))]
    count = len(chunks)
    hops, swaps, pooled, pooled_other, stages = [], [], [], [], []

    def part(k, groups):
        first, size = firsts[k] // TILE, chunks[k] // TILE
        return live[groups] - first, seg[groups, first : first + size].reshape(-1)

    near, across = slice(0, 2), slice(2, 4)
    for k in range(count + 1):
        if k < count:
            block = dense(own_lens, hidden, *weights, *norms, firsts[k], chunks[k], TILE)
            if k >= 2:
                block = tie(block, (hops[k - 2], pooled[k - 3]) if k >= 3 else hops[k - 2])
            hop = (lax.ppermute(block, "vocab", NEAR), lax.ppermute(block, "vocab", FAR))
            hops.append(hop)
            swapped = tie(hop, swaps[k - 2]) if k >= 2 else hop
            swaps.append(tuple(lax.ppermute(x, "vocab", ACROSS) for x in swapped))
        found, arrays = [], []
        if k < count:
            found.append(part(k, near))
            arrays += hops[k]
        if k > 0:
            found.append(part(k - 1, across))
            arrays += swaps[k - 1]
        alive = jnp.concatenate([f[0] for f in found])
        segs = jnp.concatenate([f[1] for f in found])
        stages.append((alive, segs, arrays))
        pooled.append(pool(alive, segs, arrays, vocabulary_weight, quad, TILE, width // 2))
    for alive, segs, arrays in stages:
        pooled_other.append(pool(alive, segs, arrays, other_weight, quad, TILE, width // 2))

    vectors_other, sent_other = finish(
        jnp.stack([shard ^ 2, upper]).astype(jnp.int32), pooled_other, other_bias[None], places[1 - own], owners, capacity
    )
    received = lax.ppermute(vectors_other, "vocab", BESIDE)
    vectors, sent = finish(
        jnp.stack([shard, upper]).astype(jnp.int32), pooled, vocabulary_bias[None], places[own], owners, capacity
    )
    got = exchange(jnp.concatenate([sent, sent_other], axis=0))
    lanes = jnp.arange(owners, dtype=jnp.int32) ^ 2
    weights_table = got[:capacity] + got[capacity:][:, lanes]
    low = jnp.where(upper == 0, vectors, received)
    high = jnp.where(upper == 0, received, vectors)
    return jnp.concatenate([low, high], axis=0), weights_table


def local(
    hidden,
    dense_w,
    dense_b,
    norm_gain,
    norm_bias,
    vocabulary_weight,
    vocabulary_bias,
    lengths,
    term_ids,
):
    passages = lengths.shape[0]
    width = vocabulary_weight.shape[1]
    vocab_count = lax.axis_size("vocab")
    batch_count = lax.axis_size("batch")
    owners = vocab_count * batch_count
    capacity = 3 * passages * K // (2 * vocab_count * owners) + 2
    shard = lax.axis_index("vocab")
    batch = lax.axis_index("batch")
    quads = vocab_count == 8 and batch_count == 4

    ids = term_ids.T
    where = jnp.stack([shard, batch * passages]).astype(jnp.int32)
    own_places, send_keys = slots(where, ids, owners, capacity, width, True)
    got_keys = exchange(send_keys)
    places = [own_places]
    if quads:
        where = jnp.stack([shard ^ 2, batch * passages]).astype(jnp.int32)
        places.append(slots(where, ids, owners, capacity, width, False)[0])
    plan = quad_plan if quads else gather_plan
    vectors, got_weights = plan(
        hidden,
        (dense_w, dense_b[None]),
        (norm_gain[None], norm_bias[None]),
        vocabulary_weight,
        vocabulary_bias,
        lengths,
        places,
        0,
        owners,
        capacity,
    )
    return vectors, got_weights[None], got_keys[None]


def solution(mesh):
    in_specs = (
        P(("batch", "vocab"), None),
        P(),
        P(),
        P(),
        P(),
        P(None, "vocab"),
        P("vocab"),
        P("batch"),
        P("batch", None),
    )
    out_specs = (
        P("batch", "vocab"),
        P(("batch", "vocab"), None, None),
        P(("batch", "vocab"), None, None),
    )
    return jax.shard_map(local, mesh=mesh, in_specs=in_specs, out_specs=out_specs, check_vma=False)
```
